32 devices in a mesh: groups: 2 (over y), tok: 4 (over x, core), head: 4 (over z).
Axes of the slice: x: 2, y: 2, z: 4, core: 2. Of those that a mesh axis runs over, the one named last changes fastest.
Arguments:
- keys: bfloat16 [24576, 1280], P(('groups', 'tok'), 'head'), parts along dimension 0, may hold values from -6 to 6
- values: bfloat16 [24576, 1280], P(('groups', 'tok'), 'head'), parts along dimension 0, may hold values from -6 to 6
- rates: float32 [24576, 4], P(('groups', 'tok'), 'head'), parts along dimension 0, may hold values from 0.5 to 4
- fast_init: bfloat16 [4, 3, 320, 320], P('head'), may hold values from -6 to 6
- samples: bfloat16 [512, 5120], P('groups', 'tok'), parts along dimension 0, may hold values from -6 to 6
- w_query: bfloat16 [5120, 1280], P('tok', 'head'), may hold values from -0.078125 to 0.078125
- w_output: bfloat16 [1280, 5120], P('head', 'tok'), may hold values from -0.15625 to 0.15625
Outputs:
- mixed: bfloat16 [512, 5120], P(('groups', 'head'), 'tok'), parts along dimension 0
- fast_new: bfloat16 [8, 3, 320, 320], P(('groups', 'head')), parts along dimension 0
The draws below stay inside these ranges and needn't reach their ends.
There are 2 independent parts, one for each index of `groups`. The reference program is written for one: setup_inputs(seed, part) draws one part's arguments, and reference() takes and returns one part's arrays. A program takes and returns all parts, laid end to end along the dimension named above; an argument that names none is the same for every part. Nothing has to cross between parts.
All inputs are finite; a program needn't handle non-finite values.
Results may differ from the reference program's by a relative error of at most 0.012.
Values may be sent and summed in bfloat16 or wider, within the bound.
A program may use at most 64 MiB of HBM per device.

```python
import math
import jax
import jax.numpy as jnp
from jax import lax

D = 5120
HD = 320
HEADS = 4
PROMPT = 12288
SAMPLES = 256


def steps_of(key, extent, split, smallest, high):
    def one(axis_at, shards_of):
        heights = jax.random.uniform(jax.random.fold_in(jax.random.fold_in(key, 6), axis_at), (shards_of,), jnp.float32, smallest / len(split), high / len(split))
        return jnp.repeat(jnp.exp(heights), extent[axis_at] // shards_of).reshape((-1,) + (1,) * (len(extent) - axis_at - 1))

    factor_of = one(*split[0])
    for cut in split[1:]:
        factor_of = factor_of * one(*cut)
    return factor_of


def centred(stream_key, dims, scale, limit, cuts=(), held_as=jnp.bfloat16):
    level = steps_of(stream_key, dims, cuts, -0.22, 0.18) if cuts else 1.0
    result = jax.random.normal(stream_key, dims, jnp.float32) * scale * level
    return jnp.minimum(jnp.maximum(result, -limit), limit).astype(held_as)


def setup_inputs(seed: int = 0, part: int = 0) -> dict:
    splits = jax.random.split(jax.random.key(seed), 8)
    part_keys = jax.random.split(jax.random.fold_in(splits[7], part), 8)
    keys = centred(part_keys[0], (PROMPT, HEADS * HD), 1.0, 6.0, ((0, 4), (1, 4)))
    values = centred(part_keys[1], (PROMPT, HEADS * HD), 1.0, 6.0, ((0, 4), (1, 4)))
    rates = jnp.clip(jnp.exp(math.log(4.0) - 2.0794415 * jax.random.uniform(part_keys[2], (PROMPT, HEADS), jnp.float32) ** steps_of(part_keys[2], (PROMPT, HEADS), ((0, 4), (1, 4)), -0.2, 0.2)), 0.5, 4.0)
    fast_init = centred(splits[3], (HEADS, 3, HD, HD), 1.0, 6.0, ((0, 4),))
    samples = centred(part_keys[4], (SAMPLES, D), 1.0, 6.0, ((1, 4),))
    w_query = centred(splits[5], (D, HEADS * HD), D ** -0.5, 0.078125, ((0, 4), (1, 4)))
    w_output = centred(splits[6], (HEADS * HD, D), (HEADS * HD) ** -0.5, 0.15625, ((0, 4), (1, 4)))
    return dict(keys=keys, values=values, rates=rates, fast_init=fast_init, samples=samples, w_query=w_query, w_output=w_output)


def unit_rows(block):
    wide = block.astype(jnp.float32)
    return (wide * lax.rsqrt(lax.optimization_barrier(jnp.sum(wide * wide, axis=-1, keepdims=True)) + 1e-06)).astype(jnp.bfloat16)

def head_gradient(operands):
    head_keys, head_values, head_rates, weights = operands
    normed = unit_rows(head_keys)
    pre_gate = jnp.dot(normed, weights[0], preferred_element_type=jnp.float32)
    pre_up = jnp.dot(normed, weights[1], preferred_element_type=jnp.float32)
    gate_sigmoid = jax.nn.sigmoid(pre_gate)
    activated = pre_gate * gate_sigmoid
    hidden = (activated * pre_up).astype(jnp.bfloat16)
    scaled = (head_rates[:, None] * head_values.astype(jnp.float32)).astype(jnp.bfloat16)
    hidden_grad = jnp.dot(scaled, weights[2].T, preferred_element_type=jnp.float32)
    gate_grad = (hidden_grad * pre_up * gate_sigmoid * (1.0 + pre_gate * (1.0 - gate_sigmoid))).astype(jnp.bfloat16)
    up_grad = (hidden_grad * activated).astype(jnp.bfloat16)
    first = jnp.dot(normed.T, gate_grad, preferred_element_type=jnp.float32)
    second = jnp.dot(normed.T, up_grad, preferred_element_type=jnp.float32)
    third = jnp.dot(hidden.T, scaled, preferred_element_type=jnp.float32)
    return jnp.stack([first, second, third])

def renorm(weights, gradient):
    former = weights.astype(jnp.float32)
    updated = former + gradient
    factor = jnp.sqrt((lax.optimization_barrier(jnp.mean(former * former, axis=-1, keepdims=True)) + 1e-05) / (lax.optimization_barrier(jnp.mean(updated * updated, axis=-1, keepdims=True)) + 1e-05))
    return (updated * factor).astype(jnp.bfloat16)

def fast_apply(normed, weights):
    wide = normed.astype(jnp.float32)
    sample_gate = jnp.einsum('shd,hde->she', wide, weights[:, 0].astype(jnp.float32))
    sample_up = jnp.einsum('shd,hde->she', wide, weights[:, 1].astype(jnp.float32))
    sample_hidden = (jax.nn.silu(sample_gate) * sample_up).astype(jnp.bfloat16)
    fast_out = jnp.einsum('shd,hde->she', sample_hidden.astype(jnp.float32), weights[:, 2].astype(jnp.float32))
    return (fast_out * lax.rsqrt(lax.optimization_barrier(jnp.mean(fast_out * fast_out, axis=-1, keepdims=True)) + 1e-05)).astype(jnp.bfloat16)

def reference(keys, values, rates, fast_init, samples, w_query, w_output):
    head_keys = jnp.moveaxis(keys.reshape(PROMPT, HEADS, HD), 1, 0)
    head_values = jnp.moveaxis(values.reshape(PROMPT, HEADS, HD), 1, 0)
    gradient = lax.map(head_gradient, (head_keys, head_values, rates.T, fast_init))
    gradient = gradient * PROMPT ** (-0.5)
    fast_new = renorm(fast_init, gradient)
    queries = jnp.dot(samples, w_query, preferred_element_type=jnp.float32)
    normed_queries = unit_rows(queries.reshape(SAMPLES, HEADS, HD))
    normed_out = fast_apply(normed_queries, fast_new)
    mixed = jnp.dot(normed_out.reshape(SAMPLES, HEADS * HD), w_output, preferred_element_type=jnp.float32)
    return (mixed.astype(jnp.bfloat16), fast_new)
```

```python
import functools

import jax
import jax.numpy as jnp
from jax import lax
from jax.experimental import pallas as pl
from jax.experimental.pallas import tpu as pltpu
from jax.sharding import PartitionSpec as P

MESH = pl.DeviceIdType.MESH
F32 = jnp.float32
BF16 = jnp.bfloat16


def dot(a, b):
    return jnp.dot(a, b, preferred_element_type=F32)


def dot_tn(a, b):
    return lax.dot_general(a, b, (((0,), (0,)), ((), ())), preferred_element_type=F32)


def dot_nt(a, b):
    return lax.dot_general(a, b, (((1,), (1,)), ((), ())), preferred_element_type=F32)


def sigmoid(v):
    return 0.5 * jnp.tanh(0.5 * v) + 0.5


def kernel(
    n_tok, n_head, chunks, step_scale,
    keys_h, values_h, rates_h, init_h, samples_h, wq_h, wo_h,
    mixed_ref, fast_h,
    keys_v, values_v, rates_v, init_v, samples_v, wq_v, wo_v, wo_pair,
    w13, w2, acc12, acc3, crecv12, crecv3, xbuf, fnew,
    qsend, qrecv, nq, nout, nrecv, tsend, trecv,
    load_sem, chunk_sem, wo_sem, q_ssem, q_rsem, c_ssem, c_rsem,
    x_ssem, x_rsem, f_ssem, f_rsem, out_sem, n_ssem, n_rsem, t_ssem, t_rsem,
):
    t = lax.axis_index("tok")
    h = lax.axis_index("head")
    n_x = n_tok // 2
    n_pair = n_head // 2
    x = t // 2
    core = lax.rem(t, 2)
    par = lax.rem(h, 2)
    pair = h // 2
    core_peer = {"tok": 2 * x + 1 - core}
    head_peer = {"head": 2 * pair + 1 - par}
    tok_peers = [{"tok": lax.rem(t + d, n_tok)} for d in range(1, n_tok)]
    x_peers = [{"tok": 2 * lax.rem(x + d, n_x) + core} for d in range(1, n_x)]
    pair_of = [lax.rem(pair + o, n_pair) for o in range(n_pair)]
    par_peers = [{"head": 2 * pair_of[o] + par} for o in range(1, n_pair)]

    barrier = pltpu.get_barrier_semaphore()
    everyone = tok_peers + [head_peer] + par_peers
    for peer in everyone:
        pl.semaphore_signal(barrier, inc=1, device_id=peer, device_id_type=MESH)

    loads = [
        pltpu.make_async_copy(samples_h, samples_v, load_sem.at[0]),
        pltpu.make_async_copy(wq_h, wq_v, load_sem.at[1]),
        pltpu.make_async_copy(init_h.at[0], init_v, load_sem.at[2]),
    ]
    rows = keys_h.shape[0] // chunks

    def chunk_copies(i):
        at = pl.ds(pl.multiple_of(i * rows, rows), rows)
        return [
            pltpu.make_async_copy(keys_h.at[at], keys_v.at[at], chunk_sem.at[0, i]),
            pltpu.make_async_copy(values_h.at[at], values_v.at[at], chunk_sem.at[1, i]),
            pltpu.make_async_copy(rates_h.at[at], rates_v.at[at], chunk_sem.at[2, i]),
        ]

    for load in loads:
        load.start()
    for i in range(chunks):
        for c in chunk_copies(i):
            c.start()
    wo_load = pltpu.make_async_copy(wo_h, wo_v, load_sem.at[3])
    wo_load.start()

    acc12[...] = jnp.zeros_like(acc12)
    acc3[...] = jnp.zeros_like(acc3)
    w13[...] = jnp.zeros_like(w13)

    hd = fnew.shape[1]
    wide = w2.shape[0]
    half = hd // 2

    loads[0].wait()
    loads[1].wait()
    queries = dot(samples_v[...], wq_v[...])
    qsend[...] = queries.astype(BF16)

    pl.semaphore_wait(barrier, len(everyone))

    wo_swap = pltpu.make_async_remote_copy(
        src_ref=wo_h, dst_ref=wo_pair, send_sem=wo_sem.at[0], recv_sem=wo_sem.at[1],
        device_id=head_peer, device_id_type=MESH,
    )
    wo_swap.start()
    q_copies = []
    for d, peer in enumerate(tok_peers):
        q_copies.append(pltpu.make_async_remote_copy(
            src_ref=qsend, dst_ref=qrecv.at[d], send_sem=q_ssem.at[d], recv_sem=q_rsem.at[d],
            device_id=peer, device_id_type=MESH,
        ))
        q_copies[-1].start()

    loads[2].wait()
    w13[:, :hd] = init_v[0]
    w13[:, wide : wide + hd] = init_v[1]
    w2[:hd, :] = init_v[2]
    w2[hd:, :] = jnp.zeros((wide - hd, hd), BF16)

    def body(i, carry):
        for c in chunk_copies(i):
            c.wait()
        at = pl.ds(pl.multiple_of(i * rows, rows), rows)
        k = keys_v[at, :].astype(F32)
        normed = (k * lax.rsqrt(jnp.sum(k * k, axis=-1, keepdims=True) + 1e-06)).astype(BF16)
        pre = dot(normed, w13[...])
        gate, up = pre[:, :wide], pre[:, wide:]
        scaled = (rates_v[at, :] * values_v[at, :].astype(F32)).astype(BF16)
        hidden_grad = dot_nt(scaled, w2[...])
        s = sigmoid(gate)
        a = gate * s
        hidden = (a * up).astype(BF16)
        gate_grad = (hidden_grad * up * (s + a * (1.0 - s))).astype(BF16)
        up_grad = (hidden_grad * a).astype(BF16)
        acc12[...] += dot_tn(normed, jnp.concatenate([gate_grad, up_grad], axis=1))
        acc3[...] += dot_tn(hidden[:, :hd], scaled)
        return carry

    lax.fori_loop(0, chunks, body, 0)

    theirs = pl.ds(pl.multiple_of(half * (1 - core), half), half)
    mine = pl.ds(pl.multiple_of(half * core, half), half)
    c_copies = [
        pltpu.make_async_remote_copy(
            src_ref=acc12.at[theirs], dst_ref=crecv12, send_sem=c_ssem.at[0],
            recv_sem=c_rsem.at[0], device_id=core_peer, device_id_type=MESH,
        ),
        pltpu.make_async_remote_copy(
            src_ref=acc3.at[theirs], dst_ref=crecv3, send_sem=c_ssem.at[1],
            recv_sem=c_rsem.at[1], device_id=core_peer, device_id_type=MESH,
        ),
    ]
    for c in c_copies:
        c.start()

    for c in q_copies:
        c.wait_recv()
    for d in range(n_tok - 1):
        queries = queries + qrecv[d].astype(F32)
    nq[...] = (
        queries * lax.rsqrt(jnp.sum(queries * queries, axis=-1, keepdims=True) + 1e-06)
    ).astype(BF16)

    c_copies[0].wait_recv()
    s12 = acc12[mine, :] + crecv12[...]
    xbuf[x, 0] = s12[:, :hd].astype(BF16)
    xbuf[x, 1] = s12[:, wide : wide + hd].astype(BF16)
    c_copies[1].wait_recv()
    xbuf[x, 2] = (acc3[mine, :] + crecv3[...]).astype(BF16)
    x_copies = []
    for d, peer in enumerate(x_peers):
        x_copies.append(pltpu.make_async_remote_copy(
            src_ref=xbuf.at[x], dst_ref=xbuf.at[x], send_sem=x_ssem.at[d], recv_sem=x_rsem.at[d],
            device_id=peer, device_id_type=MESH,
        ))
        x_copies[-1].start()
    for c in x_copies:
        c.wait_recv()

    f_copies = []
    for m in range(3):
        total = xbuf[0, m].astype(F32)
        for j in range(1, n_x):
            total = total + xbuf[j, m].astype(F32)
        former = init_v[m, mine, :].astype(F32)
        updated = former + total * step_scale
        factor = jnp.sqrt(
            (jnp.mean(former * former, axis=-1, keepdims=True) + 1e-05)
            / (jnp.mean(updated * updated, axis=-1, keepdims=True) + 1e-05)
        )
        fnew[m, mine, :] = (updated * factor).astype(BF16)
        f_copies.append(pltpu.make_async_remote_copy(
            src_ref=fnew.at[m, mine], dst_ref=fnew.at[m, mine], send_sem=f_ssem.at[m],
            recv_sem=f_rsem.at[m], device_id=core_peer, device_id_type=MESH,
        ))
        f_copies[-1].start()

    normed_q = nq[...]
    f_copies[0].wait_recv()
    gate = dot(normed_q, fnew[0])
    f_copies[1].wait_recv()
    up = dot(normed_q, fnew[1])
    sample_hidden = (gate * sigmoid(gate) * up).astype(BF16)
    f_copies[2].wait_recv()
    out_copy = pltpu.make_async_copy(fnew, fast_h.at[0], out_sem)
    out_copy.start()
    fast_out = dot(sample_hidden, fnew[2])
    normed_out = (
        fast_out * lax.rsqrt(jnp.mean(fast_out * fast_out, axis=-1, keepdims=True) + 1e-05)
    ).astype(BF16)
    block = nout.shape[1]
    for d in range(n_head):
        nout[d] = normed_out[d * block : (d + 1) * block]

    n_copies = []
    for j in range(n_pair):
        n_copies.append(pltpu.make_async_remote_copy(
            src_ref=nout.at[2 * j + 1 - par], dst_ref=nrecv.at[j], send_sem=n_ssem.at[j],
            recv_sem=n_rsem.at[j], device_id=head_peer, device_id_type=MESH,
        ))
        n_copies[-1].start()
    wo_load.wait()
    wo_swap.wait_recv()
    for c in n_copies:
        c.wait_recv()

    def terms(o):
        j = pair_of[o]
        return dot(nout[2 * j + par], wo_v[...]) + dot(nrecv[j], wo_pair[...])

    t_copies = []
    for o in range(1, n_pair):
        tsend[o - 1] = terms(o).astype(BF16)
        t_copies.append(pltpu.make_async_remote_copy(
            src_ref=tsend.at[o - 1], dst_ref=trecv.at[o - 1], send_sem=t_ssem.at[o - 1],
            recv_sem=t_rsem.at[o - 1], device_id=par_peers[o - 1], device_id_type=MESH,
        ))
        t_copies[-1].start()
    mixed = terms(0)
    for o, c in enumerate(t_copies):
        c.wait_recv()
        mixed = mixed + trecv[o].astype(F32)
    mixed_ref[...] = mixed.astype(BF16)

    out_copy.wait()
    for c in [wo_swap] + q_copies + c_copies + x_copies + f_copies + n_copies + t_copies:
        c.wait_send()


def shards(n_tok, n_head, keys, values, rates, fast_init, samples, w_query, w_output):
    tokens = keys.shape[0]
    hd = fast_init.shape[2]
    wide = -(-hd // 128) * 128
    chunks = 4
    srows = samples.shape[0]
    block = srows // n_head
    cols = w_output.shape[1]
    n_x, n_pair = n_tok // 2, n_head // 2
    dma = pltpu.SemaphoreType.DMA
    others = max(n_pair - 1, 1)
    body = functools.partial(
        kernel, n_tok, n_head, chunks, float(tokens * n_tok) ** (-0.5)
    )
    anywhere = pl.BlockSpec(memory_space=pl.ANY)
    return pl.pallas_call(
        body,
        out_shape=(
            jax.ShapeDtypeStruct((block, cols), BF16),
            jax.ShapeDtypeStruct((1, 3, hd, hd), BF16),
        ),
        in_specs=[anywhere] * 7,
        out_specs=(pl.BlockSpec(memory_space=pltpu.VMEM), anywhere),
        scratch_shapes=[
            pltpu.VMEM(keys.shape, BF16),
            pltpu.VMEM(values.shape, BF16),
            pltpu.VMEM(rates.shape, F32),
            pltpu.VMEM((3, hd, hd), BF16),
            pltpu.VMEM(samples.shape, BF16),
            pltpu.VMEM(w_query.shape, BF16),
            pltpu.VMEM(w_output.shape, BF16),
            pltpu.VMEM(w_output.shape, BF16),
            pltpu.VMEM((hd, 2 * wide), BF16),
            pltpu.VMEM((wide, hd), BF16),
            pltpu.VMEM((hd, 2 * wide), F32),
            pltpu.VMEM((hd, hd), F32),
            pltpu.VMEM((hd // 2, 2 * wide), F32),
            pltpu.VMEM((hd // 2, hd), F32),
            pltpu.VMEM((n_x, 3, hd // 2, hd), BF16),
            pltpu.VMEM((3, hd, hd), BF16),
            pltpu.VMEM((srows, hd), BF16),
            pltpu.VMEM((n_tok - 1, srows, hd), BF16),
            pltpu.VMEM((srows, hd), BF16),
            pltpu.VMEM((n_head, block, hd), BF16),
            pltpu.VMEM((n_pair, block, hd), BF16),
            pltpu.VMEM((others, block, cols), BF16),
            pltpu.VMEM((others, block, cols), BF16),
            dma((4,)),
            dma((3, chunks)),
            dma((2,)),
            dma((n_tok - 1,)),
            dma((n_tok - 1,)),
            dma((2,)),
            dma((2,)),
            dma((max(n_x - 1, 1),)),
            dma((max(n_x - 1, 1),)),
            dma((3,)),
            dma((3,)),
            dma(()),
            dma((n_pair,)),
            dma((n_pair,)),
            dma((others,)),
            dma((others,)),
        ],
        compiler_params=pltpu.CompilerParams(
            collective_id=0, has_side_effects=True, vmem_limit_bytes=56 << 20
        ),
    )(keys, values, rates, fast_init, samples, w_query, w_output)


def solution(mesh):
    return jax.shard_map(
        functools.partial(shards, mesh.shape["tok"], mesh.shape["head"]),
        mesh=mesh,
        in_specs=(
            P(("groups", "tok"), "head"),
            P(("groups", "tok"), "head"),
            P(("groups", "tok"), "head"),
            P("head", None, None, None),
            P("groups", "tok"),
            P("tok", "head"),
            P("head", "tok"),
        ),
        out_specs=(P(("groups", "head"), "tok"), P(("groups", "head"), None, None, None)),
        check_vma=False,
    )
```

```python
import functools

import jax
import jax.numpy as jnp
from jax import lax
from jax.experimental import pallas as pl
from jax.experimental.pallas import tpu as pltpu
from jax.sharding import PartitionSpec as P

MESH = pl.DeviceIdType.MESH
F32 = jnp.float32
BF16 = jnp.bfloat16


def dot(a, b):
    return jnp.dot(a, b, preferred_element_type=F32)


def dot_tn(a, b):
    return lax.dot_general(a, b, (((0,), (0,)), ((), ())), preferred_element_type=F32)


def dot_nt(a, b):
    return lax.dot_general(a, b, (((1,), (1,)), ((), ())), preferred_element_type=F32)


def sigmoid(v):
    return 0.5 * jnp.tanh(0.5 * v) + 0.5


def pack(block):
    r, hd = block.shape
    full = hd // 128
    parts = [block[:, 128 * i : 128 * (i + 1)] for i in range(full)]
    tail = block[:, 128 * full :]
    parts.append(jnp.concatenate([tail[: r // 2], tail[r // 2 :]], axis=1))
    return parts


def unpack(rows_of, r, hd):
    full = hd // 128
    parts = [rows_of(i * r, r) for i in range(full)]
    tail = rows_of(full * r, r // 2)
    parts.append(jnp.concatenate([tail[:, :64], tail[:, 64:]], axis=0))
    return jnp.concatenate(parts, axis=1)


def kernel(
    n_tok, n_head, chunks, step_scale,
    keys_h, values_h, rates_h, init_h, samples_h, wq_h, wo_h,
    mixed_ref, fast_h,
    keys_v, values_v, rates_v, init_v, samples_v, wq_v, wo_v, wo_pair,
    w13, normed_v, scaled_v, hidden_v, gate_v, up_v, acc, crecv, xbuf, fnew,
    qbuf, qpeer, qx, nq, nout, nrecv, tsend, trecv,
    load_sem, chunk_sem, wo_sem, q_sem, qx_ssem, qx_rsem, c_ssem, c_rsem,
    x_ssem, x_rsem, f_ssem, f_rsem, out_sem, n_ssem, n_rsem, t_ssem, t_rsem,
):
    t = lax.axis_index("tok")
    h = lax.axis_index("head")
    n_x = n_tok // 2
    n_pair = n_head // 2
    x = t // 2
    core = lax.rem(t, 2)
    par = lax.rem(h, 2)
    pair = h // 2
    core_peer = {"tok": 2 * x + 1 - core}
    head_peer = {"head": 2 * pair + 1 - par}
    x_peers = [{"tok": 2 * lax.rem(x + d, n_x) + core} for d in range(1, n_x)]
    pair_of = [lax.rem(pair + o, n_pair) for o in range(n_pair)]
    par_peers = [{"head": 2 * pair_of[o] + par} for o in range(1, n_pair)]

    barrier = pltpu.get_barrier_semaphore()
    everyone = [core_peer, head_peer] + x_peers + par_peers
    for peer in everyone:
        pl.semaphore_signal(barrier, inc=1, device_id=peer, device_id_type=MESH)

    sends = []

    def send(src, dst, ssem, rsem, peer):
        copy = pltpu.make_async_remote_copy(
            src_ref=src, dst_ref=dst, send_sem=ssem, recv_sem=rsem,
            device_id=peer, device_id_type=MESH,
        )
        copy.start()
        sends.append(copy)
        return copy

    rows = keys_h.shape[1] // chunks

    def chunk_copies(i):
        at = pl.ds(i * rows, rows)
        return [
            pltpu.make_async_copy(keys_h.at[:, at], keys_v.at[:, at], chunk_sem.at[0, i]),
            pltpu.make_async_copy(values_h.at[:, at], values_v.at[:, at], chunk_sem.at[1, i]),
        ]

    loads = [
        pltpu.make_async_copy(samples_h, samples_v, load_sem.at[0]),
        pltpu.make_async_copy(wq_h, wq_v, load_sem.at[1]),
        pltpu.make_async_copy(init_h.at[0], init_v, load_sem.at[2]),
        pltpu.make_async_copy(rates_h, rates_v, load_sem.at[3]),
        pltpu.make_async_copy(wo_h, wo_v, load_sem.at[4]),
    ]
    for load in loads[:4]:
        load.start()
    for i in range(chunks):
        for c in chunk_copies(i):
            c.start()
    loads[4].start()

    hd = fnew.shape[1]
    half = hd // 2
    qrows = nq.shape[1]

    loads[0].wait()
    loads[1].wait()
    queries = dot_nt(samples_v[...], wq_v[...])
    qbuf[0] = queries[:qrows]
    qbuf[1] = queries[qrows:]

    pl.semaphore_wait(barrier, len(everyone))

    q_core = send(qbuf.at[1 - core], qpeer, q_sem.at[0], q_sem.at[1], core_peer)
    wo_swap = send(wo_h, wo_pair, wo_sem.at[0], wo_sem.at[1], head_peer)

    loads[2].wait()
    w13[:hd] = init_v[0].T
    w13[hd:] = init_v[1].T
    loads[3].wait()

    q_x = []
    q_last = None
    for i in range(chunks):
        for c in chunk_copies(i):
            c.wait()
        at = pl.ds(i * rows, rows)
        k = keys_v[:, at].astype(F32)
        normed = (k * lax.rsqrt(jnp.sum(k * k, axis=0, keepdims=True) + 1e-06)).astype(BF16)
        normed_v[:, at] = normed
        pre = dot(w13[...], normed)
        gate, up = pre[:hd], pre[hd:]
        scaled = (rates_v[:, at] * values_v[:, at].astype(F32)).astype(BF16)
        scaled_v[:, at] = scaled
        hidden_grad = dot(init_v[2], scaled)
        s = sigmoid(gate)
        a = gate * s
        hidden_v[:, at] = (a * up).astype(BF16)
        gate_v[:, at] = (hidden_grad * up * (s + a * (1.0 - s))).astype(BF16)
        up_v[:, at] = (hidden_grad * a).astype(BF16)
        if i == 0:
            q_core.wait_recv()
            qx[x] = qbuf[core] + qpeer[...]
            for d, peer in enumerate(x_peers):
                q_x.append(send(qx.at[x], qx.at[x], qx_ssem.at[d], qx_rsem.at[d], peer))
        if i == chunks - 1:
            for c in q_x:
                c.wait_recv()
            queries = qx[0]
            for j in range(1, n_x):
                queries = queries + qx[j]
            nq[core] = (
                queries
                * lax.rsqrt(jnp.sum(queries * queries, axis=-1, keepdims=True) + 1e-06)
            ).astype(BF16)
            q_last = send(nq.at[core], nq.at[core], q_sem.at[2], q_sem.at[3], core_peer)

    factors = ((normed_v, gate_v), (normed_v, up_v), (hidden_v, scaled_v))
    theirs = pl.ds(pl.multiple_of(half * (1 - core), half), half)
    mine = pl.ds(pl.multiple_of(half * core, half), half)
    c_copies, x_copies = [], []

    def chip_sum(m):
        c_copies[m].wait_recv()
        total = (acc[m, mine, :] + crecv[m]).astype(BF16)
        at = 0
        for part in pack(total):
            xbuf[m, x, at : at + part.shape[0], :] = part
            at += part.shape[0]
        x_copies.append([
            send(xbuf.at[m, x], xbuf.at[m, x], x_ssem.at[m, d], x_rsem.at[m, d], peer)
            for d, peer in enumerate(x_peers)
        ])

    for m in range(3):
        acc[m] = dot_nt(factors[m][0][...], factors[m][1][...])
        c_copies.append(
            send(acc.at[m, theirs], crecv.at[m], c_ssem.at[m], c_rsem.at[m], core_peer)
        )
        if m:
            chip_sum(m - 1)
    chip_sum(2)

    f_copies = []
    for m in range(3):
        for c in x_copies[m]:
            c.wait_recv()
        total = unpack(lambda at, r: xbuf[m, 0, at : at + r, :].astype(F32), half, hd)
        for j in range(1, n_x):
            total = total + unpack(
                lambda at, r: xbuf[m, j, at : at + r, :].astype(F32), half, hd
            )
        former = init_v[m, mine, :].astype(F32)
        updated = former + total * step_scale
        factor = jnp.sqrt(
            (jnp.mean(former * former, axis=-1, keepdims=True) + 1e-05)
            / (jnp.mean(updated * updated, axis=-1, keepdims=True) + 1e-05)
        )
        fnew[m, mine, :] = (updated * factor).astype(BF16)
        f_copies.append(send(
            fnew.at[m, mine], fnew.at[m, mine], f_ssem.at[m], f_rsem.at[m], core_peer
        ))
        if m == 0:
            q_last.wait_recv()
            normed_q = nq[...].reshape(2 * qrows, hd)
        if m == 1:
            f_copies[0].wait_recv()
            gate = dot(normed_q, fnew[0])
            gate = gate * sigmoid(gate)
        if m == 2:
            f_copies[1].wait_recv()
            sample_hidden = (gate * dot(normed_q, fnew[1])).astype(BF16)
    f_copies[2].wait_recv()
    out_copy = pltpu.make_async_copy(fnew, fast_h.at[0], out_sem)
    out_copy.start()
    fast_out = dot(sample_hidden, fnew[2])
    normed_out = (
        fast_out * lax.rsqrt(jnp.mean(fast_out * fast_out, axis=-1, keepdims=True) + 1e-05)
    ).astype(BF16)
    block = nout.shape[1]
    for d in range(n_head):
        nout[d] = normed_out[d * block : (d + 1) * block]

    n_copies = [
        send(nout.at[2 * j + 1 - par], nrecv.at[j], n_ssem.at[j], n_rsem.at[j], head_peer)
        for j in range(n_pair)
    ]
    loads[4].wait()
    wo_swap.wait_recv()
    own = [dot(nout[2 * pair_of[o] + par], wo_v[...]) for o in range(n_pair)]
    for c in n_copies:
        c.wait_recv()
    t_copies = []
    for o in range(1, n_pair):
        tsend[o - 1] = (own[o] + dot(nrecv[pair_of[o]], wo_pair[...])).astype(BF16)
        t_copies.append(send(
            tsend.at[o - 1], trecv.at[o - 1], t_ssem.at[o - 1], t_rsem.at[o - 1],
            par_peers[o - 1],
        ))
    mixed = own[0] + dot(nrecv[pair], wo_pair[...])
    for o, c in enumerate(t_copies):
        c.wait_recv()
        mixed = mixed + trecv[o].astype(F32)
    mixed_ref[...] = mixed.astype(BF16)

    out_copy.wait()
    for c in sends:
        c.wait_send()


def copy_out(mixed_ref, fast_ref, mixed_out, fast_out, sem):
    copies = [
        pltpu.make_async_copy(mixed_ref, mixed_out, sem.at[0]),
        pltpu.make_async_copy(fast_ref, fast_out, sem.at[1]),
    ]
    for c in copies:
        c.start()
    for c in copies:
        c.wait()


def shards(n_tok, n_head, keys, values, rates, fast_init, samples, w_query, w_output):
    tokens = keys.shape[0]
    hd = fast_init.shape[2]
    chunks = 4
    srows = samples.shape[0]
    block = srows // n_head
    cols = w_output.shape[1]
    n_x, n_pair = n_tok // 2, n_head // 2
    dma = pltpu.SemaphoreType.DMA
    others = max(n_pair - 1, 1)
    other_x = max(n_x - 1, 1)
    body = functools.partial(
        kernel, n_tok, n_head, chunks, float(tokens * n_tok) ** (-0.5)
    )
    anywhere = pl.BlockSpec(memory_space=pl.ANY)
    vmem = pltpu.VMEM
    packed = (hd // 2) * hd // 128
    outs = (
        jax.ShapeDtypeStruct((block, cols), BF16),
        jax.ShapeDtypeStruct((1, 3, hd, hd), BF16),
    )
    mixed, fast_new = pl.pallas_call(
        body,
        out_shape=outs,
        in_specs=[anywhere] * 7,
        out_specs=(pl.BlockSpec(memory_space=pltpu.VMEM), anywhere),
        scratch_shapes=[
            vmem((hd, tokens), BF16),
            vmem((hd, tokens), BF16),
            vmem((1, tokens), F32),
            vmem((3, hd, hd), BF16),
            vmem(samples.shape, BF16),
            vmem((hd, w_query.shape[0]), BF16),
            vmem(w_output.shape, BF16),
            vmem(w_output.shape, BF16),
            vmem((2 * hd, hd), BF16),
            vmem((hd, tokens), BF16),
            vmem((hd, tokens), BF16),
            vmem((hd, tokens), BF16),
            vmem((hd, tokens), BF16),
            vmem((hd, tokens), BF16),
            vmem((3, hd, hd), F32),
            vmem((3, hd // 2, hd), F32),
            vmem((3, n_x, packed, 128), BF16),
            vmem((3, hd, hd), BF16),
            vmem((2, srows // 2, hd), F32),
            vmem((srows // 2, hd), F32),
            vmem((n_x, srows // 2, hd), F32),
            vmem((2, srows // 2, hd), BF16),
            vmem((n_head, block, hd), BF16),
            vmem((n_pair, block, hd), BF16),
            vmem((others, block, cols), BF16),
            vmem((others, block, cols), BF16),
            dma((5,)),
            dma((2, chunks)),
            dma((2,)),
            dma((4,)),
            dma((other_x,)),
            dma((other_x,)),
            dma((3,)),
            dma((3,)),
            dma((3, other_x)),
            dma((3, other_x)),
            dma((3,)),
            dma((3,)),
            dma(()),
            dma((n_pair,)),
            dma((n_pair,)),
            dma((others,)),
            dma((others,)),
        ],
        compiler_params=pltpu.CompilerParams(
            collective_id=0, has_side_effects=True, vmem_limit_bytes=56 << 20
        ),
    )(keys.T, values.T, rates.T, fast_init, samples, w_query.T, w_output)
    return pl.pallas_call(
        copy_out,
        out_shape=outs,
        in_specs=[anywhere] * 2,
        out_specs=(anywhere, anywhere),
        scratch_shapes=[dma((2,))],
    )(mixed, fast_new)


def solution(mesh):
    return jax.shard_map(
        functools.partial(shards, mesh.shape["tok"], mesh.shape["head"]),
        mesh=mesh,
        in_specs=(
            P(("groups", "tok"), "head"),
            P(("groups", "tok"), "head"),
            P(("groups", "tok"), "head"),
            P("head", None, None, None),
            P("groups", "tok"),
            P("tok", "head"),
            P("head", "tok"),
        ),
        out_specs=(P(("groups", "head"), "tok"), P(("groups", "head"), None, None, None)),
        check_vma=False,
    )
```

```python
import functools

import jax
import jax.numpy as jnp
from jax import lax
from jax.experimental import pallas as pl
from jax.experimental.pallas import tpu as pltpu
from jax.sharding import PartitionSpec as P

MESH = pl.DeviceIdType.MESH
F32 = jnp.float32
BF16 = jnp.bfloat16


def dot(a, b):
    return jnp.dot(a, b, preferred_element_type=F32)


def dot_tn(a, b):
    return lax.dot_general(a, b, (((0,), (0,)), ((), ())), preferred_element_type=F32)


def dot_nt(a, b):
    return lax.dot_general(a, b, (((1,), (1,)), ((), ())), preferred_element_type=F32)


def sigmoid(v):
    return 0.5 * jnp.tanh(0.5 * v) + 0.5


def pack(block):
    r, hd = block.shape
    full = hd // 128
    parts = [block[:, 128 * i : 128 * (i + 1)] for i in range(full)]
    tail = block[:, 128 * full :]
    parts.append(jnp.concatenate([tail[: r // 2], tail[r // 2 :]], axis=1))
    return parts


def unpack(rows_of, r, hd):
    full = hd // 128
    parts = [rows_of(i * r, r) for i in range(full)]
    tail = rows_of(full * r, r // 2)
    parts.append(jnp.concatenate([tail[:, :64], tail[:, 64:]], axis=0))
    return jnp.concatenate(parts, axis=1)


def kernel(
    n_tok, n_head, chunks, step_scale,
    keys_h, values_h, rates_h, init_h, samples_h, wq_h, wo_h,
    mixed_ref, fast_h,
    keys_v, values_v, rates_v, init_v, samples_v, wq_v, wo_v, wo_pair,
    w13, normed_v, scaled_v, hidden_v, gate_v, up_v, acc, crecv, xbuf, fnew,
    qbuf, qpeer, qx, nq, nout, nrecv, tsend, trecv,
    load_sem, chunk_sem, wo_sem, q_sem, qx_ssem, qx_rsem, c_ssem, c_rsem,
    x_ssem, x_rsem, f_ssem, f_rsem, out_sem, n_ssem, n_rsem, t_ssem, t_rsem,
):
    t = lax.axis_index("tok")
    h = lax.axis_index("head")
    n_x = n_tok // 2
    n_pair = n_head // 2
    x = t // 2
    core = lax.rem(t, 2)
    par = lax.rem(h, 2)
    pair = h // 2
    core_peer = {"tok": 2 * x + 1 - core}
    head_peer = {"head": 2 * pair + 1 - par}
    x_peers = [{"tok": 2 * lax.rem(x + d, n_x) + core} for d in range(1, n_x)]
    pair_of = [lax.rem(pair + o, n_pair) for o in range(n_pair)]
    par_peers = [{"head": 2 * pair_of[o] + par} for o in range(1, n_pair)]

    barrier = pltpu.get_barrier_semaphore()
    everyone = [core_peer, head_peer] + x_peers + par_peers
    for peer in everyone:
        pl.semaphore_signal(barrier, inc=1, device_id=peer, device_id_type=MESH)

    sends = []

    def send(src, dst, ssem, rsem, peer):
        copy = pltpu.make_async_remote_copy(
            src_ref=src, dst_ref=dst, send_sem=ssem, recv_sem=rsem,
            device_id=peer, device_id_type=MESH,
        )
        copy.start()
        sends.append(copy)
        return copy

    rows = keys_h.shape[1] // chunks

    def chunk_copies(i):
        at = pl.ds(i * rows, rows)
        return [
            pltpu.make_async_copy(keys_h.at[:, at], keys_v.at[:, at], chunk_sem.at[0, i]),
            pltpu.make_async_copy(values_h.at[:, at], values_v.at[:, at], chunk_sem.at[1, i]),
        ]

    loads = [
        pltpu.make_async_copy(samples_h, samples_v, load_sem.at[0]),
        pltpu.make_async_copy(wq_h, wq_v, load_sem.at[1]),
        pltpu.make_async_copy(init_h.at[0], init_v, load_sem.at[2]),
        pltpu.make_async_copy(rates_h, rates_v, load_sem.at[3]),
        pltpu.make_async_copy(wo_h, wo_v, load_sem.at[4]),
    ]
    for load in loads[:4]:
        load.start()
    for i in range(chunks):
        for c in chunk_copies(i):
            c.start()
    loads[4].start()

    hd = fnew.shape[1]
    half = hd // 2
    qrows = nq.shape[1]

    loads[0].wait()
    loads[1].wait()
    queries = dot_nt(samples_v[...], wq_v[...])
    qbuf[0] = queries[:qrows]
    qbuf[1] = queries[qrows:]

    pl.semaphore_wait(barrier, len(everyone))

    q_core = send(qbuf.at[1 - core], qpeer, q_sem.at[0], q_sem.at[1], core_peer)
    wo_swap = send(wo_h, wo_pair, wo_sem.at[0], wo_sem.at[1], head_peer)

    loads[2].wait()
    w13[:hd] = init_v[0].T
    w13[hd:] = init_v[1].T
    loads[3].wait()

    q_x = []
    q_last = None
    for i in range(chunks):
        for c in chunk_copies(i):
            c.wait()
        at = pl.ds(i * rows, rows)
        k = keys_v[:, at].astype(F32)
        normed = (k * lax.rsqrt(jnp.sum(k * k, axis=0, keepdims=True) + 1e-06)).astype(BF16)
        normed_v[:, at] = normed
        pre = dot(w13[...], normed)
        gate, up = pre[:hd], pre[hd:]
        scaled = (rates_v[:, at] * values_v[:, at].astype(F32)).astype(BF16)
        scaled_v[:, at] = scaled
        hidden_grad = dot(init_v[2], scaled)
        s = sigmoid(gate)
        a = gate * s
        hidden_v[:, at] = (a * up).astype(BF16)
        gate_v[:, at] = (hidden_grad * up * (s + a * (1.0 - s))).astype(BF16)
        up_v[:, at] = (hidden_grad * a).astype(BF16)
        if i == 0:
            q_core.wait_recv()
            qx[x] = qbuf[core] + qpeer[...]
            for d, peer in enumerate(x_peers):
                q_x.append(send(qx.at[x], qx.at[x], qx_ssem.at[d], qx_rsem.at[d], peer))
        if i == chunks - 1:
            for c in q_x:
                c.wait_recv()
            queries = qx[0]
            for j in range(1, n_x):
                queries = queries + qx[j]
            nq[core] = (
                queries
                * lax.rsqrt(jnp.sum(queries * queries, axis=-1, keepdims=True) + 1e-06)
            ).astype(BF16)
            q_last = send(nq.at[core], nq.at[core], q_sem.at[2], q_sem.at[3], core_peer)

    factors = ((normed_v, gate_v), (normed_v, up_v), (hidden_v, scaled_v))
    theirs = pl.ds(pl.multiple_of(half * (1 - core), half), half)
    mine = pl.ds(pl.multiple_of(half * core, half), half)
    c_copies, x_copies = [], []

    def chip_sum(m):
        c_copies[m].wait_recv()
        total = (acc[m, mine, :] + crecv[m]).astype(BF16)
        at = 0
        for part in pack(total):
            xbuf[m, x, at : at + part.shape[0], :] = part
            at += part.shape[0]
        x_copies.append([
            send(xbuf.at[m, x], xbuf.at[m, x], x_ssem.at[m, d], x_rsem.at[m, d], peer)
            for d, peer in enumerate(x_peers)
        ])

    for m in range(3):
        acc[m] = dot_nt(factors[m][0][...], factors[m][1][...])
        c_copies.append(
            send(acc.at[m, theirs], crecv.at[m], c_ssem.at[m], c_rsem.at[m], core_peer)
        )
        if m:
            chip_sum(m - 1)
    chip_sum(2)

    f_copies = []
    for m in range(3):
        for c in x_copies[m]:
            c.wait_recv()
        total = unpack(lambda at, r: xbuf[m, 0, at : at + r, :].astype(F32), half, hd)
        for j in range(1, n_x):
            total = total + unpack(
                lambda at, r: xbuf[m, j, at : at + r, :].astype(F32), half, hd
            )
        former = init_v[m, mine, :].astype(F32)
        updated = former + total * step_scale
        factor = jnp.sqrt(
            (jnp.mean(former * former, axis=-1, keepdims=True) + 1e-05)
            / (jnp.mean(updated * updated, axis=-1, keepdims=True) + 1e-05)
        )
        fnew[m, mine, :] = (updated * factor).astype(BF16)
        f_copies.append(send(
            fnew.at[m, mine], fnew.at[m, mine], f_ssem.at[m], f_rsem.at[m], core_peer
        ))
        if m == 0:
            q_last.wait_recv()
            normed_q = nq[...].reshape(2 * qrows, hd)
        if m == 1:
            f_copies[0].wait_recv()
            gate = dot(normed_q, fnew[0])
            gate = gate * sigmoid(gate)
        if m == 2:
            f_copies[1].wait_recv()
            sample_hidden = (gate * dot(normed_q, fnew[1])).astype(BF16)
    f_copies[2].wait_recv()
    out_copy = pltpu.make_async_copy(fnew, fast_h.at[0], out_sem)
    out_copy.start()
    fast_out = dot(sample_hidden, fnew[2])
    normed_out = (
        fast_out * lax.rsqrt(jnp.mean(fast_out * fast_out, axis=-1, keepdims=True) + 1e-05)
    ).astype(BF16)
    block = nout.shape[1]
    for d in range(n_head):
        nout[d] = normed_out[d * block : (d + 1) * block]

    n_copies = [
        send(nout.at[2 * j + 1 - par], nrecv.at[j], n_ssem.at[j], n_rsem.at[j], head_peer)
        for j in range(n_pair)
    ]
    loads[4].wait()
    wo_swap.wait_recv()
    own = [dot(nout[2 * pair_of[o] + par], wo_v[...]) for o in range(n_pair)]
    for c in n_copies:
        c.wait_recv()
    t_copies = []
    for o in range(1, n_pair):
        tsend[o - 1] = (own[o] + dot(nrecv[pair_of[o]], wo_pair[...])).astype(BF16)
        t_copies.append(send(
            tsend.at[o - 1], trecv.at[o - 1], t_ssem.at[o - 1], t_rsem.at[o - 1],
            par_peers[o - 1],
        ))
    mixed = own[0] + dot(nrecv[pair], wo_pair[...])
    for o, c in enumerate(t_copies):
        c.wait_recv()
        mixed = mixed + trecv[o].astype(F32)
    mixed_ref[...] = mixed.astype(BF16)

    out_copy.wait()
    for c in sends:
        c.wait_send()


def copy_out(mixed_ref, fast_ref, mixed_out, fast_out):
    mixed_out[...] = mixed_ref[...]
    fast_out[...] = fast_ref[...]


def shards(n_tok, n_head, keys, values, rates, fast_init, samples, w_query, w_output):
    tokens = keys.shape[0]
    hd = fast_init.shape[2]
    chunks = 4
    srows = samples.shape[0]
    block = srows // n_head
    cols = w_output.shape[1]
    n_x, n_pair = n_tok // 2, n_head // 2
    dma = pltpu.SemaphoreType.DMA
    others = max(n_pair - 1, 1)
    other_x = max(n_x - 1, 1)
    body = functools.partial(
        kernel, n_tok, n_head, chunks, float(tokens * n_tok) ** (-0.5)
    )
    anywhere = pl.BlockSpec(memory_space=pl.ANY)
    whole = pl.BlockSpec(memory_space=pltpu.VMEM)
    vmem = pltpu.VMEM
    packed = (hd // 2) * hd // 128
    outs = (
        jax.ShapeDtypeStruct((block, cols), BF16),
        jax.ShapeDtypeStruct((1, 3, hd, hd), BF16),
    )
    mixed, fast_new = pl.pallas_call(
        body,
        out_shape=outs,
        in_specs=[anywhere] * 7,
        out_specs=(pl.BlockSpec(memory_space=pltpu.VMEM), anywhere),
        scratch_shapes=[
            vmem((hd, tokens), BF16),
            vmem((hd, tokens), BF16),
            vmem((1, tokens), F32),
            vmem((3, hd, hd), BF16),
            vmem(samples.shape, BF16),
            vmem((hd, w_query.shape[0]), BF16),
            vmem(w_output.shape, BF16),
            vmem(w_output.shape, BF16),
            vmem((2 * hd, hd), BF16),
            vmem((hd, tokens), BF16),
            vmem((hd, tokens), BF16),
            vmem((hd, tokens), BF16),
            vmem((hd, tokens), BF16),
            vmem((hd, tokens), BF16),
            vmem((3, hd, hd), F32),
            vmem((3, hd // 2, hd), F32),
            vmem((3, n_x, packed, 128), BF16),
            vmem((3, hd, hd), BF16),
            vmem((2, srows // 2, hd), F32),
            vmem((srows // 2, hd), F32),
            vmem((n_x, srows // 2, hd), F32),
            vmem((2, srows // 2, hd), BF16),
            vmem((n_head, block, hd), BF16),
            vmem((n_pair, block, hd), BF16),
            vmem((others, block, cols), BF16),
            vmem((others, block, cols), BF16),
            dma((5,)),
            dma((2, chunks)),
            dma((2,)),
            dma((4,)),
            dma((other_x,)),
            dma((other_x,)),
            dma((3,)),
            dma((3,)),
            dma((3, other_x)),
            dma((3, other_x)),
            dma((3,)),
            dma((3,)),
            dma(()),
            dma((n_pair,)),
            dma((n_pair,)),
            dma((others,)),
            dma((others,)),
        ],
        compiler_params=pltpu.CompilerParams(
            collective_id=0, has_side_effects=True, vmem_limit_bytes=56 << 20
        ),
    )(keys.T, values.T, rates.T, fast_init, samples, w_query.T, w_output)
    return pl.pallas_call(
        copy_out,
        out_shape=outs,
        in_specs=[whole] * 2,
        out_specs=(whole, whole),
    )(mixed, fast_new)


def solution(mesh):
    return jax.shard_map(
        functools.partial(shards, mesh.shape["tok"], mesh.shape["head"]),
        mesh=mesh,
        in_specs=(
            P(("groups", "tok"), "head"),
            P(("groups", "tok"), "head"),
            P(("groups", "tok"), "head"),
            P("head", None, None, None),
            P("groups", "tok"),
            P("tok", "head"),
            P("head", "tok"),
        ),
        out_specs=(P(("groups", "head"), "tok"), P(("groups", "head"), None, None, None)),
        check_vma=False,
    )
```

```python
import functools

import jax
import jax.numpy as jnp
from jax import lax
from jax.experimental import pallas as pl
from jax.experimental.pallas import tpu as pltpu
from jax.sharding import PartitionSpec as P

MESH = pl.DeviceIdType.MESH
F32 = jnp.float32
BF16 = jnp.bfloat16


def dot(a, b):
    return jnp.dot(a, b, preferred_element_type=F32)


def dot_tn(a, b):
    return lax.dot_general(a, b, (((0,), (0,)), ((), ())), preferred_element_type=F32)


def dot_nt(a, b):
    return lax.dot_general(a, b, (((1,), (1,)), ((), ())), preferred_element_type=F32)


def sigmoid(v):
    return 0.5 * jnp.tanh(0.5 * v) + 0.5


def pack(block):
    r, hd = block.shape
    full = hd // 128
    parts = [block[:, 128 * i : 128 * (i + 1)] for i in range(full)]
    tail = block[:, 128 * full :]
    parts.append(jnp.concatenate([tail[: r // 2], tail[r // 2 :]], axis=1))
    return parts


def unpack(rows_of, r, hd):
    full = hd // 128
    parts = [rows_of(i * r, r) for i in range(full)]
    tail = rows_of(full * r, r // 2)
    parts.append(jnp.concatenate([tail[:, :64], tail[:, 64:]], axis=0))
    return jnp.concatenate(parts, axis=1)


def kernel(
    n_tok, n_head, chunks, step_scale,
    keys_h, values_h, rates_h, init_h, samples_h, wq_h, wo_h,
    mixed_ref, fast_h,
    keys_v, values_v, rates_v, init_v, samples_v, wq_v, wo_v, wo_pair,
    w13, normed_v, scaled_v, hidden_v, gate_v, up_v, acc, crecv, xbuf, fnew,
    qbuf, qpeer, qx, nq, nout, nrecv, tsend, trecv,
    load_sem, chunk_sem, wo_sem, q_sem, qx_ssem, qx_rsem, c_ssem, c_rsem,
    x_ssem, x_rsem, f_ssem, f_rsem, out_sem, n_ssem, n_rsem, t_ssem, t_rsem,
):
    t = lax.axis_index("tok")
    h = lax.axis_index("head")
    n_x = n_tok // 2
    n_pair = n_head // 2
    x = t // 2
    core = lax.rem(t, 2)
    par = lax.rem(h, 2)
    pair = h // 2
    core_peer = {"tok": 2 * x + 1 - core}
    head_peer = {"head": 2 * pair + 1 - par}
    x_peers = [{"tok": 2 * lax.rem(x + d, n_x) + core} for d in range(1, n_x)]
    pair_of = [lax.rem(pair + o, n_pair) for o in range(n_pair)]
    par_peers = [{"head": 2 * pair_of[o] + par} for o in range(1, n_pair)]

    barrier = pltpu.get_barrier_semaphore()
    everyone = [core_peer, head_peer] + x_peers + par_peers
    for peer in everyone:
        pl.semaphore_signal(barrier, inc=1, device_id=peer, device_id_type=MESH)

    sends = []

    def send(src, dst, ssem, rsem, peer):
        copy = pltpu.make_async_remote_copy(
            src_ref=src, dst_ref=dst, send_sem=ssem, recv_sem=rsem,
            device_id=peer, device_id_type=MESH,
        )
        copy.start()
        sends.append(copy)
        return copy

    rows = keys_h.shape[1] // chunks

    def chunk_copies(i):
        at = pl.ds(i * rows, rows)
        return [
            pltpu.make_async_copy(keys_h.at[:, at], keys_v.at[:, at], chunk_sem.at[0, i]),
            pltpu.make_async_copy(values_h.at[:, at], values_v.at[:, at], chunk_sem.at[1, i]),
        ]

    loads = [
        pltpu.make_async_copy(samples_h, samples_v, load_sem.at[0]),
        pltpu.make_async_copy(wq_h, wq_v, load_sem.at[1]),
        pltpu.make_async_copy(init_h.at[0], init_v, load_sem.at[2]),
        pltpu.make_async_copy(rates_h, rates_v, load_sem.at[3]),
        pltpu.make_async_copy(wo_h, wo_v, load_sem.at[4]),
    ]
    for load in loads[:4]:
        load.start()
    for i in range(chunks):
        for c in chunk_copies(i):
            c.start()
    loads[4].start()

    hd = fnew.shape[1]
    half = hd // 2
    qrows = qpeer.shape[0]
    group = nq.shape[2]

    loads[0].wait()
    loads[1].wait()
    queries = dot_nt(samples_v[...], wq_v[...])
    qbuf[0] = queries[:qrows]
    qbuf[1] = queries[qrows:]

    pl.semaphore_wait(barrier, len(everyone))

    q_core = send(qbuf.at[1 - core], qpeer, q_sem.at[0], q_sem.at[1], core_peer)
    wo_swap = send(wo_h, wo_pair, wo_sem.at[0], wo_sem.at[1], head_peer)

    loads[2].wait()
    w13[:hd] = init_v[0].T
    w13[hd:] = init_v[1].T
    loads[3].wait()

    q_x = []
    q_last = None
    for i in range(chunks):
        for c in chunk_copies(i):
            c.wait()
        at = pl.ds(i * rows, rows)
        k = keys_v[:, at].astype(F32)
        normed = (k * lax.rsqrt(jnp.sum(k * k, axis=0, keepdims=True) + 1e-06)).astype(BF16)
        normed_v[:, at] = normed
        pre = dot(w13[...], normed)
        gate, up = pre[:hd], pre[hd:]
        scaled = (rates_v[:, at] * values_v[:, at].astype(F32)).astype(BF16)
        scaled_v[:, at] = scaled
        hidden_grad = dot(init_v[2], scaled)
        s = sigmoid(gate)
        a = gate * s
        hidden_v[:, at] = (a * up).astype(BF16)
        gate_v[:, at] = (hidden_grad * up * (s + a * (1.0 - s))).astype(BF16)
        up_v[:, at] = (hidden_grad * a).astype(BF16)
        if i == 0:
            q_core.wait_recv()
            qx[x] = qbuf[core] + qpeer[...]
            for d, peer in enumerate(x_peers):
                q_x.append(send(qx.at[x], qx.at[x], qx_ssem.at[d], qx_rsem.at[d], peer))
        if i == chunks - 1:
            for c in q_x:
                c.wait_recv()
            queries = qx[0]
            for j in range(1, n_x):
                queries = queries + qx[j]
            normed_q = (
                queries
                * lax.rsqrt(jnp.sum(queries * queries, axis=-1, keepdims=True) + 1e-06)
            ).astype(BF16)
            for j in range(nq.shape[1]):
                nq[core, j] = normed_q[j * group : (j + 1) * group]
            q_last = send(nq.at[core], nq.at[core], q_sem.at[2], q_sem.at[3], core_peer)

    factors = ((normed_v, gate_v), (normed_v, up_v), (hidden_v, scaled_v))
    theirs = pl.ds(pl.multiple_of(half * (1 - core), half), half)
    mine = pl.ds(pl.multiple_of(half * core, half), half)
    c_copies, x_copies = [], []

    def chip_sum(m):
        c_copies[m].wait_recv()
        total = (acc[m, mine, :] + crecv[m]).astype(BF16)
        at = 0
        for part in pack(total):
            xbuf[m, x, at : at + part.shape[0], :] = part
            at += part.shape[0]
        x_copies.append([
            send(xbuf.at[m, x], xbuf.at[m, x], x_ssem.at[m, d], x_rsem.at[m, d], peer)
            for d, peer in enumerate(x_peers)
        ])

    for m in range(3):
        acc[m] = dot_nt(factors[m][0][...], factors[m][1][...])
        c_copies.append(
            send(acc.at[m, theirs], crecv.at[m], c_ssem.at[m], c_rsem.at[m], core_peer)
        )
        if m:
            chip_sum(m - 1)
    chip_sum(2)

    f_copies = []
    for m in range(3):
        for c in x_copies[m]:
            c.wait_recv()
        total = unpack(lambda at, r: xbuf[m, 0, at : at + r, :].astype(F32), half, hd)
        for j in range(1, n_x):
            total = total + unpack(
                lambda at, r: xbuf[m, j, at : at + r, :].astype(F32), half, hd
            )
        former = init_v[m, mine, :].astype(F32)
        updated = former + total * step_scale
        factor = jnp.sqrt(
            (jnp.mean(former * former, axis=-1, keepdims=True) + 1e-05)
            / (jnp.mean(updated * updated, axis=-1, keepdims=True) + 1e-05)
        )
        fnew[m, mine, :] = (updated * factor).astype(BF16)
        f_copies.append(send(
            fnew.at[m, mine], fnew.at[m, mine], f_ssem.at[m], f_rsem.at[m], core_peer
        ))
        if m == 0:
            q_last.wait_recv()

    order = list(range(1, n_pair)) + [0]
    per_half = nq.shape[1]
    block = group // 2
    gates, hiddens = [], []
    normed_q = [nq[pair_of[o] // per_half, lax.rem(pair_of[o], per_half)] for o in order]
    f_copies[0].wait_recv()
    for rows_q in normed_q:
        gate = dot(rows_q, fnew[0])
        gates.append(gate * sigmoid(gate))
    f_copies[1].wait_recv()
    for gate, rows_q in zip(gates, normed_q):
        hiddens.append((gate * dot(rows_q, fnew[1])).astype(BF16))
    f_copies[2].wait_recv()
    out_copy = pltpu.make_async_copy(fnew, fast_h.at[0], out_sem)
    out_copy.start()
    n_copies = {}
    for o, sample_hidden in zip(order, hiddens):
        fast_out = dot(sample_hidden, fnew[2])
        normed_out = (
            fast_out * lax.rsqrt(jnp.mean(fast_out * fast_out, axis=-1, keepdims=True) + 1e-05)
        ).astype(BF16)
        nout[o, 0] = normed_out[:block]
        nout[o, 1] = normed_out[block:]
        n_copies[o] = send(
            nout.at[o, 1 - par], nrecv.at[o], n_ssem.at[o], n_rsem.at[o], head_peer
        )

    loads[4].wait()
    wo_swap.wait_recv()
    parts = tsend.shape[1]
    width = tsend.shape[3]

    def terms(o, p):
        at = slice(p * width, (p + 1) * width)
        return dot(nout[o, par], wo_v[:, at]) + dot(nrecv[o], wo_pair[:, at])

    t_copies = {}
    for o in range(1, n_pair):
        n_copies[o].wait_recv()
        for p in range(parts):
            tsend[o - 1, p] = terms(o, p).astype(BF16)
            t_copies[o, p] = send(
                tsend.at[o - 1, p], trecv.at[o - 1, p], t_ssem.at[o - 1, p],
                t_rsem.at[o - 1, p], par_peers[o - 1],
            )
    n_copies[0].wait_recv()
    mixed = [terms(0, p) for p in range(parts)]
    for p in range(parts):
        for o in range(1, n_pair):
            t_copies[o, p].wait_recv()
            mixed[p] = mixed[p] + trecv[o - 1, p].astype(F32)
        mixed_ref[:, p * width : (p + 1) * width] = mixed[p].astype(BF16)

    out_copy.wait()
    for c in sends:
        c.wait_send()


def copy_out(mixed_ref, fast_ref, mixed_out, fast_out):
    mixed_out[...] = mixed_ref[...]
    fast_out[...] = fast_ref[...]


def shards(n_tok, n_head, keys, values, rates, fast_init, samples, w_query, w_output):
    tokens = keys.shape[0]
    hd = fast_init.shape[2]
    chunks = 4
    srows = samples.shape[0]
    block = srows // n_head
    cols = w_output.shape[1]
    n_x, n_pair = n_tok // 2, n_head // 2
    dma = pltpu.SemaphoreType.DMA
    others = max(n_pair - 1, 1)
    parts = cols // 256 if cols % 256 == 0 else 1
    other_x = max(n_x - 1, 1)
    body = functools.partial(
        kernel, n_tok, n_head, chunks, float(tokens * n_tok) ** (-0.5)
    )
    anywhere = pl.BlockSpec(memory_space=pl.ANY)
    whole = pl.BlockSpec(memory_space=pltpu.VMEM)
    vmem = pltpu.VMEM
    packed = (hd // 2) * hd // 128
    outs = (
        jax.ShapeDtypeStruct((block, cols), BF16),
        jax.ShapeDtypeStruct((1, 3, hd, hd), BF16),
    )
    mixed, fast_new = pl.pallas_call(
        body,
        out_shape=outs,
        in_specs=[anywhere] * 7,
        out_specs=(pl.BlockSpec(memory_space=pltpu.VMEM), anywhere),
        scratch_shapes=[
            vmem((hd, tokens), BF16),
            vmem((hd, tokens), BF16),
            vmem((1, tokens), F32),
            vmem((3, hd, hd), BF16),
            vmem(samples.shape, BF16),
            vmem((hd, w_query.shape[0]), BF16),
            vmem(w_output.shape, BF16),
            vmem(w_output.shape, BF16),
            vmem((2 * hd, hd), BF16),
            vmem((hd, tokens), BF16),
            vmem((hd, tokens), BF16),
            vmem((hd, tokens), BF16),
            vmem((hd, tokens), BF16),
            vmem((hd, tokens), BF16),
            vmem((3, hd, hd), F32),
            vmem((3, hd // 2, hd), F32),
            vmem((3, n_x, packed, 128), BF16),
            vmem((3, hd, hd), BF16),
            vmem((2, srows // 2, hd), F32),
            vmem((srows // 2, hd), F32),
            vmem((n_x, srows // 2, hd), F32),
            vmem((2, n_pair // 2, 2 * block, hd), BF16),
            vmem((n_pair, 2, block, hd), BF16),
            vmem((n_pair, block, hd), BF16),
            vmem((others, parts, block, cols // parts), BF16),
            vmem((others, parts, block, cols // parts), BF16),
            dma((5,)),
            dma((2, chunks)),
            dma((2,)),
            dma((4,)),
            dma((other_x,)),
            dma((other_x,)),
            dma((3,)),
            dma((3,)),
            dma((3, other_x)),
            dma((3, other_x)),
            dma((3,)),
            dma((3,)),
            dma(()),
            dma((n_pair,)),
            dma((n_pair,)),
            dma((others, parts)),
            dma((others, parts)),
        ],
        compiler_params=pltpu.CompilerParams(
            collective_id=0, has_side_effects=True, vmem_limit_bytes=56 << 20
        ),
    )(keys.T, values.T, rates.T, fast_init, samples, w_query.T, w_output)
    return pl.pallas_call(
        copy_out,
        out_shape=outs,
        in_specs=[whole] * 2,
        out_specs=(whole, whole),
    )(mixed, fast_new)


def solution(mesh):
    return jax.shard_map(
        functools.partial(shards, mesh.shape["tok"], mesh.shape["head"]),
        mesh=mesh,
        in_specs=(
            P(("groups", "tok"), "head"),
            P(("groups", "tok"), "head"),
            P(("groups", "tok"), "head"),
            P("head", None, None, None),
            P("groups", "tok"),
            P("tok", "head"),
            P("head", "tok"),
        ),
        out_specs=(P(("groups", "head"), "tok"), P(("groups", "head"), None, None, None)),
        check_vma=False,
    )
```

```python
import functools

import jax
import jax.numpy as jnp
from jax import lax
from jax.experimental import pallas as pl
from jax.experimental.pallas import tpu as pltpu
from jax.sharding import PartitionSpec as P

MESH = pl.DeviceIdType.MESH
F32 = jnp.float32
BF16 = jnp.bfloat16


def dot(a, b):
    return jnp.dot(a, b, preferred_element_type=F32)


def dot_tn(a, b):
    return lax.dot_general(a, b, (((0,), (0,)), ((), ())), preferred_element_type=F32)


def dot_nt(a, b):
    return lax.dot_general(a, b, (((1,), (1,)), ((), ())), preferred_element_type=F32)


def sigmoid(v):
    return 0.5 * jnp.tanh(0.5 * v) + 0.5


def pack(block):
    r, hd = block.shape
    full = hd // 128
    parts = [block[:, 128 * i : 128 * (i + 1)] for i in range(full)]
    tail = block[:, 128 * full :]
    parts.append(jnp.concatenate([tail[: r // 2], tail[r // 2 :]], axis=1))
    return parts


def unpack(rows_of, r, hd):
    full = hd // 128
    parts = [rows_of(i * r, r) for i in range(full)]
    tail = rows_of(full * r, r // 2)
    parts.append(jnp.concatenate([tail[:, :64], tail[:, 64:]], axis=0))
    return jnp.concatenate(parts, axis=1)


def kernel(
    n_tok, n_head, chunks, step_scale,
    keys_h, values_h, rates_h, init_h, samples_h, wq_h, wo_h,
    mixed_ref, fast_h,
    keys_v, values_v, rates_v, init_v, samples_v, wq_v, wo_v, wo_pair,
    w13, normed_v, scaled_v, hidden_v, gate_v, up_v, acc, crecv, xbuf, fnew,
    qbuf, qpeer, qx, nq, nout, nrecv, tsend, trecv,
    load_sem, chunk_sem, wo_sem, q_sem, qx_ssem, qx_rsem, c_ssem, c_rsem,
    x_ssem, x_rsem, f_ssem, f_rsem, out_sem, n_ssem, n_rsem, t_ssem, t_rsem,
):
    t = lax.axis_index("tok")
    h = lax.axis_index("head")
    n_x = n_tok // 2
    n_pair = n_head // 2
    x = t // 2
    core = lax.rem(t, 2)
    par = lax.rem(h, 2)
    pair = h // 2
    core_peer = {"tok": 2 * x + 1 - core}
    head_peer = {"head": 2 * pair + 1 - par}
    x_peers = [{"tok": 2 * lax.rem(x + d, n_x) + core} for d in range(1, n_x)]
    pair_of = [lax.rem(pair + o, n_pair) for o in range(n_pair)]
    par_peers = [{"head": 2 * pair_of[o] + par} for o in range(1, n_pair)]

    barrier = pltpu.get_barrier_semaphore()
    everyone = [core_peer, head_peer] + x_peers + par_peers
    for peer in everyone:
        pl.semaphore_signal(barrier, inc=1, device_id=peer, device_id_type=MESH)

    sends = []

    def send(src, dst, ssem, rsem, peer):
        copy = pltpu.make_async_remote_copy(
            src_ref=src, dst_ref=dst, send_sem=ssem, recv_sem=rsem,
            device_id=peer, device_id_type=MESH,
        )
        copy.start()
        sends.append(copy)
        return copy

    rows = keys_h.shape[1] // chunks

    def chunk_copies(i):
        at = pl.ds(i * rows, rows)
        return [
            pltpu.make_async_copy(keys_h.at[:, at], keys_v.at[:, at], chunk_sem.at[0, i]),
            pltpu.make_async_copy(values_h.at[:, at], values_v.at[:, at], chunk_sem.at[1, i]),
        ]

    loads = [
        pltpu.make_async_copy(samples_h, samples_v, load_sem.at[0]),
        pltpu.make_async_copy(wq_h, wq_v, load_sem.at[1]),
        pltpu.make_async_copy(init_h.at[0], init_v, load_sem.at[2]),
        pltpu.make_async_copy(rates_h, rates_v, load_sem.at[3]),
        pltpu.make_async_copy(wo_h, wo_v, load_sem.at[4]),
    ]
    for load in loads[:4]:
        load.start()
    for i in range(chunks):
        for c in chunk_copies(i):
            c.start()
    loads[4].start()

    hd = fnew.shape[1]
    half = hd // 2
    qrows = qpeer.shape[0]
    group = nq.shape[2]

    loads[0].wait()
    loads[1].wait()
    queries = dot_nt(samples_v[...], wq_v[...])
    qbuf[0] = queries[:qrows]
    qbuf[1] = queries[qrows:]

    pl.semaphore_wait(barrier, len(everyone))

    q_core = send(qbuf.at[1 - core], qpeer, q_sem.at[0], q_sem.at[1], core_peer)
    wo_swap = send(wo_h, wo_pair, wo_sem.at[0], wo_sem.at[1], head_peer)

    loads[2].wait()
    w13[:hd] = init_v[0].T
    w13[hd:] = init_v[1].T
    loads[3].wait()

    q_x = []
    q_last = None
    for i in range(chunks):
        for c in chunk_copies(i):
            c.wait()
        at = pl.ds(i * rows, rows)
        k = keys_v[:, at].astype(F32)
        normed = (k * lax.rsqrt(jnp.sum(k * k, axis=0, keepdims=True) + 1e-06)).astype(BF16)
        normed_v[:, at] = normed
        pre = dot(w13[...], normed)
        gate, up = pre[:hd], pre[hd:]
        scaled = (rates_v[:, at] * values_v[:, at].astype(F32)).astype(BF16)
        scaled_v[:, at] = scaled
        hidden_grad = dot(init_v[2], scaled)
        s = sigmoid(gate)
        a = gate * s
        hidden_v[:, at] = (a * up).astype(BF16)
        gate_v[:, at] = (hidden_grad * up * (s + a * (1.0 - s))).astype(BF16)
        up_v[:, at] = (hidden_grad * a).astype(BF16)
        if i == 0:
            q_core.wait_recv()
            qx[x] = qbuf[core] + qpeer[...]
            for d, peer in enumerate(x_peers):
                q_x.append(send(qx.at[x], qx.at[x], qx_ssem.at[d], qx_rsem.at[d], peer))
        if i == chunks - 1:
            for c in q_x:
                c.wait_recv()
            queries = qx[0]
            for j in range(1, n_x):
                queries = queries + qx[j]
            normed_q = (
                queries
                * lax.rsqrt(jnp.sum(queries * queries, axis=-1, keepdims=True) + 1e-06)
            ).astype(BF16)
            for j in range(nq.shape[1]):
                nq[core, j] = normed_q[j * group : (j + 1) * group]
            q_last = send(nq.at[core], nq.at[core], q_sem.at[2], q_sem.at[3], core_peer)

    factors = ((normed_v, gate_v), (normed_v, up_v), (hidden_v, scaled_v))
    theirs = pl.ds(pl.multiple_of(half * (1 - core), half), half)
    mine = pl.ds(pl.multiple_of(half * core, half), half)
    c_copies, x_copies = [], []

    def chip_sum(m):
        c_copies[m].wait_recv()
        total = (acc[m, mine, :] + crecv[m]).astype(BF16)
        at = 0
        for part in pack(total):
            xbuf[m, x, at : at + part.shape[0], :] = part
            at += part.shape[0]
        x_copies.append([
            send(xbuf.at[m, x], xbuf.at[m, x], x_ssem.at[m, d], x_rsem.at[m, d], peer)
            for d, peer in enumerate(x_peers)
        ])

    for m in range(3):
        acc[m] = dot_nt(factors[m][0][...], factors[m][1][...])
        c_copies.append(
            send(acc.at[m, theirs], crecv.at[m], c_ssem.at[m], c_rsem.at[m], core_peer)
        )
        if m:
            chip_sum(m - 1)
    chip_sum(2)

    f_copies = []
    for m in range(3):
        for c in x_copies[m]:
            c.wait_recv()
        total = unpack(lambda at, r: xbuf[m, 0, at : at + r, :].astype(F32), half, hd)
        for j in range(1, n_x):
            total = total + unpack(
                lambda at, r: xbuf[m, j, at : at + r, :].astype(F32), half, hd
            )
        former = init_v[m, mine, :].astype(F32)
        updated = former + total * step_scale
        factor = jnp.sqrt(
            (jnp.mean(former * former, axis=-1, keepdims=True) + 1e-05)
            / (jnp.mean(updated * updated, axis=-1, keepdims=True) + 1e-05)
        )
        fnew[m, mine, :] = (updated * factor).astype(BF16)
        f_copies.append(send(
            fnew.at[m, mine], fnew.at[m, mine], f_ssem.at[m], f_rsem.at[m], core_peer
        ))
        if m == 0:
            q_last.wait_recv()

    order = list(range(1, n_pair)) + [0]
    per_half = nq.shape[1]
    block = group // 2
    gates, hiddens = [], []
    normed_q = [nq[pair_of[o] // per_half, lax.rem(pair_of[o], per_half)] for o in order]
    f_copies[0].wait_recv()
    for rows_q in normed_q:
        gate = dot(rows_q, fnew[0])
        gates.append(gate * sigmoid(gate))
    f_copies[1].wait_recv()
    for gate, rows_q in zip(gates, normed_q):
        hiddens.append((gate * dot(rows_q, fnew[1])).astype(BF16))
    f_copies[2].wait_recv()
    out_copy = pltpu.make_async_copy(fnew, fast_h.at[0], out_sem)
    out_copy.start()
    n_copies = {}
    for o, sample_hidden in zip(order, hiddens):
        fast_out = dot(sample_hidden, fnew[2])
        normed_out = (
            fast_out * lax.rsqrt(jnp.mean(fast_out * fast_out, axis=-1, keepdims=True) + 1e-05)
        ).astype(BF16)
        nout[o, 0] = normed_out[:block]
        nout[o, 1] = normed_out[block:]
        n_copies[o] = send(
            nout.at[o, 1 - par], nrecv.at[o], n_ssem.at[o], n_rsem.at[o], head_peer
        )

    loads[4].wait()
    wo_swap.wait_recv()
    parts = tsend.shape[1]
    width = tsend.shape[3]

    def terms(o, p):
        at = slice(p * width, (p + 1) * width)
        return dot(nout[o, par], wo_v[:, at]) + dot(nrecv[o], wo_pair[:, at])

    t_copies = {}
    for o in range(1, n_pair):
        n_copies[o].wait_recv()
        for p in range(parts):
            tsend[o - 1, p] = terms(o, p).astype(BF16)
            t_copies[o, p] = send(
                tsend.at[o - 1, p], trecv.at[o - 1, p], t_ssem.at[o - 1, p],
                t_rsem.at[o - 1, p], par_peers[o - 1],
            )
    n_copies[0].wait_recv()
    mixed = [terms(0, p) for p in range(parts)]
    for p in range(parts):
        for o in range(1, n_pair):
            t_copies[o, p].wait_recv()
            mixed[p] = mixed[p] + trecv[o - 1, p].astype(F32)
        mixed_ref[:, p * width : (p + 1) * width] = mixed[p].astype(BF16)

    out_copy.wait()
    for c in sends:
        c.wait_send()


def copy_out(mixed_ref, fast_ref, mixed_out, fast_out, mixed_v, fast_v, sem):
    ways = [(mixed_ref, mixed_v, mixed_out)]
    ways += [(fast_ref.at[0, m], fast_v.at[m], fast_out.at[0, m]) for m in range(3)]
    loads = [pltpu.make_async_copy(w[0], w[1], sem.at[0, i]) for i, w in enumerate(ways)]
    stores = [pltpu.make_async_copy(w[1], w[2], sem.at[1, i]) for i, w in enumerate(ways)]
    for c in loads:
        c.start()
    for load, store in zip(loads, stores):
        load.wait()
        store.start()
    for c in stores:
        c.wait()


def shards(n_tok, n_head, keys, values, rates, fast_init, samples, w_query, w_output):
    tokens = keys.shape[0]
    hd = fast_init.shape[2]
    chunks = 3
    srows = samples.shape[0]
    block = srows // n_head
    cols = w_output.shape[1]
    n_x, n_pair = n_tok // 2, n_head // 2
    dma = pltpu.SemaphoreType.DMA
    others = max(n_pair - 1, 1)
    parts = cols // 256 if cols % 256 == 0 else 1
    other_x = max(n_x - 1, 1)
    body = functools.partial(
        kernel, n_tok, n_head, chunks, float(tokens * n_tok) ** (-0.5)
    )
    anywhere = pl.BlockSpec(memory_space=pl.ANY)
    vmem = pltpu.VMEM
    packed = (hd // 2) * hd // 128
    outs = (
        jax.ShapeDtypeStruct((block, cols), BF16),
        jax.ShapeDtypeStruct((1, 3, hd, hd), BF16),
    )
    mixed, fast_new = pl.pallas_call(
        body,
        out_shape=outs,
        in_specs=[anywhere] * 7,
        out_specs=(pl.BlockSpec(memory_space=pltpu.VMEM), anywhere),
        scratch_shapes=[
            vmem((hd, tokens), BF16),
            vmem((hd, tokens), BF16),
            vmem((1, tokens), F32),
            vmem((3, hd, hd), BF16),
            vmem(samples.shape, BF16),
            vmem((hd, w_query.shape[0]), BF16),
            vmem(w_output.shape, BF16),
            vmem(w_output.shape, BF16),
            vmem((2 * hd, hd), BF16),
            vmem((hd, tokens), BF16),
            vmem((hd, tokens), BF16),
            vmem((hd, tokens), BF16),
            vmem((hd, tokens), BF16),
            vmem((hd, tokens), BF16),
            vmem((3, hd, hd), F32),
            vmem((3, hd // 2, hd), F32),
            vmem((3, n_x, packed, 128), BF16),
            vmem((3, hd, hd), BF16),
            vmem((2, srows // 2, hd), F32),
            vmem((srows // 2, hd), F32),
            vmem((n_x, srows // 2, hd), F32),
            vmem((2, n_pair // 2, 2 * block, hd), BF16),
            vmem((n_pair, 2, block, hd), BF16),
            vmem((n_pair, block, hd), BF16),
            vmem((others, parts, block, cols // parts), BF16),
            vmem((others, parts, block, cols // parts), BF16),
            dma((5,)),
            dma((2, chunks)),
            dma((2,)),
            dma((4,)),
            dma((other_x,)),
            dma((other_x,)),
            dma((3,)),
            dma((3,)),
            dma((3, other_x)),
            dma((3, other_x)),
            dma((3,)),
            dma((3,)),
            dma(()),
            dma((n_pair,)),
            dma((n_pair,)),
            dma((others, parts)),
            dma((others, parts)),
        ],
        compiler_params=pltpu.CompilerParams(
            collective_id=0, has_side_effects=True, vmem_limit_bytes=56 << 20
        ),
    )(keys.T, values.T, rates.T, fast_init, samples, w_query.T, w_output)
    return pl.pallas_call(
        copy_out,
        out_shape=outs,
        in_specs=[anywhere] * 2,
        out_specs=(anywhere, anywhere),
        scratch_shapes=[vmem((block, cols), BF16), vmem((3, hd, hd), BF16), dma((2, 4))],
    )(mixed, fast_new)


def solution(mesh):
    return jax.shard_map(
        functools.partial(shards, mesh.shape["tok"], mesh.shape["head"]),
        mesh=mesh,
        in_specs=(
            P(("groups", "tok"), "head"),
            P(("groups", "tok"), "head"),
            P(("groups", "tok"), "head"),
            P("head", None, None, None),
            P("groups", "tok"),
            P("tok", "head"),
            P("head", "tok"),
        ),
        out_specs=(P(("groups", "head"), "tok"), P(("groups", "head"), None, None, None)),
        check_vma=False,
    )
```

```python
import functools

import jax
import jax.numpy as jnp
from jax import lax
from jax.experimental import pallas as pl
from jax.experimental.pallas import tpu as pltpu
from jax.sharding import PartitionSpec as P

MESH = pl.DeviceIdType.MESH
F32 = jnp.float32
BF16 = jnp.bfloat16


def dot(a, b):
    return jnp.dot(a, b, preferred_element_type=F32)


def dot_tn(a, b):
    return lax.dot_general(a, b, (((0,), (0,)), ((), ())), preferred_element_type=F32)


def dot_nt(a, b):
    return lax.dot_general(a, b, (((1,), (1,)), ((), ())), preferred_element_type=F32)


def sigmoid(v):
    return 0.5 * jnp.tanh(0.5 * v) + 0.5


def pack(block):
    r, hd = block.shape
    full = hd // 128
    parts = [block[:, 128 * i : 128 * (i + 1)] for i in range(full)]
    tail = block[:, 128 * full :]
    parts.append(jnp.concatenate([tail[: r // 2], tail[r // 2 :]], axis=1))
    return parts


def unpack(rows_of, r, hd):
    full = hd // 128
    parts = [rows_of(i * r, r) for i in range(full)]
    tail = rows_of(full * r, r // 2)
    parts.append(jnp.concatenate([tail[:, :64], tail[:, 64:]], axis=0))
    return jnp.concatenate(parts, axis=1)


def kernel(
    n_tok, n_head, chunks, step_scale,
    keys_h, values_h, rates_h, init_h, samples_h, wq_h, wo_h,
    mixed_ref, fast_h,
    keys_v, values_v, rates_v, init_v, samples_v, wq_v, wo_v, wo_pair,
    w13, normed_v, scaled_v, hidden_v, gate_v, up_v, acc, crecv, xbuf, fnew,
    qbuf, qpeer, qx, nq, nout, nrecv, tsend, trecv,
    load_sem, chunk_sem, wo_sem, q_sem, qx_ssem, qx_rsem, c_ssem, c_rsem,
    x_ssem, x_rsem, f_ssem, f_rsem, out_sem, n_ssem, n_rsem, t_ssem, t_rsem,
):
    t = lax.axis_index("tok")
    h = lax.axis_index("head")
    n_x = n_tok // 2
    n_pair = n_head // 2
    x = t // 2
    core = lax.rem(t, 2)
    par = lax.rem(h, 2)
    pair = h // 2
    core_peer = {"tok": 2 * x + 1 - core}
    head_peer = {"head": 2 * pair + 1 - par}
    x_peers = [{"tok": 2 * lax.rem(x + d, n_x) + core} for d in range(1, n_x)]
    pair_of = [lax.rem(pair + o, n_pair) for o in range(n_pair)]
    par_peers = [{"head": 2 * pair_of[o] + par} for o in range(1, n_pair)]

    barrier = pltpu.get_barrier_semaphore()
    everyone = [core_peer, head_peer] + x_peers + par_peers
    for peer in everyone:
        pl.semaphore_signal(barrier, inc=1, device_id=peer, device_id_type=MESH)

    sends = []

    def send(src, dst, ssem, rsem, peer):
        copy = pltpu.make_async_remote_copy(
            src_ref=src, dst_ref=dst, send_sem=ssem, recv_sem=rsem,
            device_id=peer, device_id_type=MESH,
        )
        copy.start()
        sends.append(copy)
        return copy

    rows = keys_h.shape[1] // chunks

    def chunk_copies(i):
        at = pl.ds(i * rows, rows)
        return [
            pltpu.make_async_copy(keys_h.at[:, at], keys_v.at[:, at], chunk_sem.at[0, i]),
            pltpu.make_async_copy(values_h.at[:, at], values_v.at[:, at], chunk_sem.at[1, i]),
        ]

    loads = [
        pltpu.make_async_copy(samples_h, samples_v, load_sem.at[0]),
        pltpu.make_async_copy(wq_h, wq_v, load_sem.at[1]),
        pltpu.make_async_copy(init_h.at[0], init_v, load_sem.at[2]),
        pltpu.make_async_copy(rates_h, rates_v, load_sem.at[3]),
        pltpu.make_async_copy(wo_h, wo_v, load_sem.at[4]),
    ]
    for load in loads[:4]:
        load.start()
    for i in range(chunks):
        for c in chunk_copies(i):
            c.start()
    loads[4].start()

    hd = fnew.shape[1]
    half = hd // 2
    qrows = qpeer.shape[0]
    group = nq.shape[2]

    loads[0].wait()
    loads[1].wait()
    queries = dot_nt(samples_v[...], wq_v[...])
    qbuf[0] = queries[:qrows]
    qbuf[1] = queries[qrows:]

    pl.semaphore_wait(barrier, len(everyone))

    q_core = send(qbuf.at[1 - core], qpeer, q_sem.at[0], q_sem.at[1], core_peer)
    wo_swap = send(wo_h, wo_pair, wo_sem.at[0], wo_sem.at[1], head_peer)

    loads[2].wait()
    w13[:hd] = init_v[0].T
    w13[hd:] = init_v[1].T
    loads[3].wait()

    q_x = []
    q_last = None
    for i in range(chunks):
        for c in chunk_copies(i):
            c.wait()
        at = pl.ds(i * rows, rows)
        k = keys_v[:, at].astype(F32)
        normed = (k * lax.rsqrt(jnp.sum(k * k, axis=0, keepdims=True) + 1e-06)).astype(BF16)
        normed_v[:, at] = normed
        pre = dot(w13[...], normed)
        gate, up = pre[:hd], pre[hd:]
        scaled = (rates_v[:, at] * values_v[:, at].astype(F32)).astype(BF16)
        scaled_v[:, at] = scaled
        hidden_grad = dot(init_v[2], scaled)
        s = sigmoid(gate)
        a = gate * s
        hidden_v[:, at] = (a * up).astype(BF16)
        gate_v[:, at] = (hidden_grad * up * (s + a * (1.0 - s))).astype(BF16)
        up_v[:, at] = (hidden_grad * a).astype(BF16)
        if i == 0:
            q_core.wait_recv()
            qx[x] = qbuf[core] + qpeer[...]
            for d, peer in enumerate(x_peers):
                q_x.append(send(qx.at[x], qx.at[x], qx_ssem.at[d], qx_rsem.at[d], peer))
        if i == chunks - 1:
            for c in q_x:
                c.wait_recv()
            queries = qx[0]
            for j in range(1, n_x):
                queries = queries + qx[j]
            normed_q = (
                queries
                * lax.rsqrt(jnp.sum(queries * queries, axis=-1, keepdims=True) + 1e-06)
            ).astype(BF16)
            for j in range(nq.shape[1]):
                nq[core, j] = normed_q[j * group : (j + 1) * group]
            q_last = send(nq.at[core], nq.at[core], q_sem.at[2], q_sem.at[3], core_peer)

    factors = ((normed_v, gate_v), (normed_v, up_v), (hidden_v, scaled_v))
    theirs = pl.ds(pl.multiple_of(half * (1 - core), half), half)
    mine = pl.ds(pl.multiple_of(half * core, half), half)
    c_copies, x_copies = [], []

    def chip_sum(m):
        c_copies[m].wait_recv()
        total = (acc[m, mine, :] + crecv[m]).astype(BF16)
        at = 0
        for part in pack(total):
            xbuf[m, x, at : at + part.shape[0], :] = part
            at += part.shape[0]
        x_copies.append([
            send(xbuf.at[m, x], xbuf.at[m, x], x_ssem.at[m, d], x_rsem.at[m, d], peer)
            for d, peer in enumerate(x_peers)
        ])

    for m in range(3):
        acc[m] = dot_nt(factors[m][0][...], factors[m][1][...])
        c_copies.append(
            send(acc.at[m, theirs], crecv.at[m], c_ssem.at[m], c_rsem.at[m], core_peer)
        )
        if m:
            chip_sum(m - 1)
    chip_sum(2)

    f_copies = []
    for m in range(3):
        for c in x_copies[m]:
            c.wait_recv()
        total = unpack(lambda at, r: xbuf[m, 0, at : at + r, :].astype(F32), half, hd)
        for j in range(1, n_x):
            total = total + unpack(
                lambda at, r: xbuf[m, j, at : at + r, :].astype(F32), half, hd
            )
        former = init_v[m, mine, :].astype(F32)
        updated = former + total * step_scale
        factor = jnp.sqrt(
            (jnp.mean(former * former, axis=-1, keepdims=True) + 1e-05)
            / (jnp.mean(updated * updated, axis=-1, keepdims=True) + 1e-05)
        )
        fnew[m, mine, :] = (updated * factor).astype(BF16)
        f_copies.append(send(
            fnew.at[m, mine], fnew.at[m, mine], f_ssem.at[m], f_rsem.at[m], core_peer
        ))
        if m == 0:
            q_last.wait_recv()

    order = list(range(1, n_pair)) + [0]
    per_half = nq.shape[1]
    block = group // 2
    gates, hiddens = [], []
    normed_q = [nq[pair_of[o] // per_half, lax.rem(pair_of[o], per_half)] for o in order]
    f_copies[0].wait_recv()
    for rows_q in normed_q:
        gate = dot(rows_q, fnew[0])
        gates.append(gate * sigmoid(gate))
    f_copies[1].wait_recv()
    for gate, rows_q in zip(gates, normed_q):
        hiddens.append((gate * dot(rows_q, fnew[1])).astype(BF16))
    f_copies[2].wait_recv()
    out_copy = pltpu.make_async_copy(fnew, fast_h.at[0], out_sem)
    out_copy.start()
    n_copies = {}
    for o, sample_hidden in zip(order, hiddens):
        fast_out = dot(sample_hidden, fnew[2])
        normed_out = (
            fast_out * lax.rsqrt(jnp.mean(fast_out * fast_out, axis=-1, keepdims=True) + 1e-05)
        ).astype(BF16)
        nout[o, 0] = normed_out[:block]
        nout[o, 1] = normed_out[block:]
        n_copies[o] = send(
            nout.at[o, 1 - par], nrecv.at[o], n_ssem.at[o], n_rsem.at[o], head_peer
        )

    loads[4].wait()
    wo_swap.wait_recv()
    parts = tsend.shape[1]
    width = tsend.shape[3]

    def terms(o, p):
        at = slice(p * width, (p + 1) * width)
        return dot(nout[o, par], wo_v[:, at]) + dot(nrecv[o], wo_pair[:, at])

    t_copies = {}
    for o in range(1, n_pair):
        n_copies[o].wait_recv()
        for p in range(parts):
            tsend[o - 1, p] = terms(o, p).astype(BF16)
            t_copies[o, p] = send(
                tsend.at[o - 1, p], trecv.at[o - 1, p], t_ssem.at[o - 1, p],
                t_rsem.at[o - 1, p], par_peers[o - 1],
            )
    n_copies[0].wait_recv()
    mixed = [terms(0, p) for p in range(parts)]
    for p in range(parts):
        for o in range(1, n_pair):
            t_copies[o, p].wait_recv()
            mixed[p] = mixed[p] + trecv[o - 1, p].astype(F32)
        mixed_ref[:, p * width : (p + 1) * width] = mixed[p].astype(BF16)

    out_copy.wait()
    for c in sends:
        c.wait_send()


def copy_out(mixed_ref, fast_ref, mixed_out, fast_out, mixed_v, fast_v, sem):
    ways = [(mixed_ref, mixed_v, mixed_out)]
    ways += [(fast_ref.at[0, m], fast_v.at[m], fast_out.at[0, m]) for m in range(3)]
    loads = [pltpu.make_async_copy(w[0], w[1], sem.at[0, i]) for i, w in enumerate(ways)]
    stores = [pltpu.make_async_copy(w[1], w[2], sem.at[1, i]) for i, w in enumerate(ways)]
    for c in loads:
        c.start()
    for load, store in zip(loads, stores):
        load.wait()
        store.start()
    for c in stores:
        c.wait()


def shards(n_tok, n_head, keys, values, rates, fast_init, samples, w_query, w_output):
    tokens = keys.shape[0]
    hd = fast_init.shape[2]
    chunks = 2
    srows = samples.shape[0]
    block = srows // n_head
    cols = w_output.shape[1]
    n_x, n_pair = n_tok // 2, n_head // 2
    dma = pltpu.SemaphoreType.DMA
    others = max(n_pair - 1, 1)
    parts = cols // 256 if cols % 256 == 0 else 1
    other_x = max(n_x - 1, 1)
    body = functools.partial(
        kernel, n_tok, n_head, chunks, float(tokens * n_tok) ** (-0.5)
    )
    anywhere = pl.BlockSpec(memory_space=pl.ANY)
    vmem = pltpu.VMEM
    packed = (hd // 2) * hd // 128
    outs = (
        jax.ShapeDtypeStruct((block, cols), BF16),
        jax.ShapeDtypeStruct((1, 3, hd, hd), BF16),
    )
    mixed, fast_new = pl.pallas_call(
        body,
        out_shape=outs,
        in_specs=[anywhere] * 7,
        out_specs=(pl.BlockSpec(memory_space=pltpu.VMEM), anywhere),
        scratch_shapes=[
            vmem((hd, tokens), BF16),
            vmem((hd, tokens), BF16),
            vmem((1, tokens), F32),
            vmem((3, hd, hd), BF16),
            vmem(samples.shape, BF16),
            vmem((hd, w_query.shape[0]), BF16),
            vmem(w_output.shape, BF16),
            vmem(w_output.shape, BF16),
            vmem((2 * hd, hd), BF16),
            vmem((hd, tokens), BF16),
            vmem((hd, tokens), BF16),
            vmem((hd, tokens), BF16),
            vmem((hd, tokens), BF16),
            vmem((hd, tokens), BF16),
            vmem((3, hd, hd), F32),
            vmem((3, hd // 2, hd), F32),
            vmem((3, n_x, packed, 128), BF16),
            vmem((3, hd, hd), BF16),
            vmem((2, srows // 2, hd), F32),
            vmem((srows // 2, hd), F32),
            vmem((n_x, srows // 2, hd), F32),
            vmem((2, n_pair // 2, 2 * block, hd), BF16),
            vmem((n_pair, 2, block, hd), BF16),
            vmem((n_pair, block, hd), BF16),
            vmem((others, parts, block, cols // parts), BF16),
            vmem((others, parts, block, cols // parts), BF16),
            dma((5,)),
            dma((2, chunks)),
            dma((2,)),
            dma((4,)),
            dma((other_x,)),
            dma((other_x,)),
            dma((3,)),
            dma((3,)),
            dma((3, other_x)),
            dma((3, other_x)),
            dma((3,)),
            dma((3,)),
            dma(()),
            dma((n_pair,)),
            dma((n_pair,)),
            dma((others, parts)),
            dma((others, parts)),
        ],
        compiler_params=pltpu.CompilerParams(
            collective_id=0, has_side_effects=True, vmem_limit_bytes=56 << 20
        ),
    )(keys.T, values.T, rates.T, fast_init, samples, w_query.T, w_output)
    return pl.pallas_call(
        copy_out,
        out_shape=outs,
        in_specs=[anywhere] * 2,
        out_specs=(anywhere, anywhere),
        scratch_shapes=[vmem((block, cols), BF16), vmem((3, hd, hd), BF16), dma((2, 4))],
    )(mixed, fast_new)


def solution(mesh):
    return jax.shard_map(
        functools.partial(shards, mesh.shape["tok"], mesh.shape["head"]),
        mesh=mesh,
        in_specs=(
            P(("groups", "tok"), "head"),
            P(("groups", "tok"), "head"),
            P(("groups", "tok"), "head"),
            P("head", None, None, None),
            P("groups", "tok"),
            P("tok", "head"),
            P("head", "tok"),
        ),
        out_specs=(P(("groups", "head"), "tok"), P(("groups", "head"), None, None, None)),
        check_vma=False,
    )
```
